512 devices in a mesh: prow: 32 (over z, core), pcol: 16 (over x, y).
Axes of the slice: x: 4, y: 4, z: 16, core: 2. Of those that a mesh axis runs over, the one named last changes fastest.
Arguments:
- factor_t: bfloat16 [4, 256, 131072], P(None, 'pcol', 'prow'), may hold values from -0.03125 to 0.03125
- pattern: int32 [512, 4], P('prow'), may hold values from 0 to 1, as said below
- diag_inverse: bfloat16 [4, 256, 256], P(None, 'pcol'), as said below
- right_side: bfloat16 [131072, 256], P(('prow', 'pcol')), may hold values from -6 to 6
- later_solution: bfloat16 [131072, 256], P(('prow', 'pcol')), may hold values from -6 to 6
Outputs:
- solution: bfloat16 [4, 256, 256], P(None, 'pcol')
- reduced: bfloat16 [131072, 256], P(('prow', 'pcol'))
The draws below stay inside these ranges and needn't reach their ends.
Inputs may be any that keep to these rules, and one draw needn't show every extreme that they name: Block row p * 16 holds the diagonal block of panel p for p < 4; its pattern is 1 exactly for the panels before p. Each diag_inverse[p] is lower triangular with a nonzero diagonal.
All inputs are finite; a program needn't handle non-finite values.
Results may differ from the reference program's by a relative error of at most 0.0047.
Values may be sent and summed in bfloat16 or wider, within the bound.
A program may use at most 64 MiB of HBM per device.

```python
import math
import jax
import jax.numpy as jnp
from jax import lax

PW = 256
PANELS = 4
RHS = 256
RB = 16
NROW = 512


def draw_pattern(key, part):
    base = jax.random.randint(key, (NROW, PANELS), 0, 4)
    row_ids = lax.broadcasted_iota(jnp.int32, (NROW, PANELS), 0)
    col_ids = lax.broadcasted_iota(jnp.int32, (NROW, PANELS), 1)
    diagonal = (row_ids % RB == 0) & (row_ids // RB < PANELS)
    return jnp.where(diagonal, (col_ids < row_ids // RB).astype(jnp.int32), (base > 0).astype(jnp.int32))


def draw_diag_inverse(key, part):
    key_off, key_diag = jax.random.split(jax.random.fold_in(key, 11))
    shape = (PANELS, PW, PW)
    below = jax.random.normal(key_off, shape, jnp.float32) / math.sqrt(PW)
    middle = jax.random.uniform(key_diag, shape, jnp.float32, 0.7, 1.4)
    row_ids = lax.broadcasted_iota(jnp.int32, shape, 1)
    col_ids = lax.broadcasted_iota(jnp.int32, shape, 2)
    return jnp.where(col_ids < row_ids, below, jnp.where(col_ids == row_ids, middle, 0.0)).astype(jnp.bfloat16)


def block_scale(key, shape, pieces, smallest, high):
    gain = 1.0
    for position, blocks in pieces:
        steps = jax.random.uniform(jax.random.fold_in(jax.random.fold_in(key, 6), position), (blocks,), jnp.float32, smallest / len(pieces), high / len(pieces))
        gain = gain * jnp.repeat(jnp.exp(steps), shape[position] // blocks).reshape((-1,) + (1,) * (len(shape) - 1 - position))
    return gain


def bell_draw(rng, dims, deviation, limit, pieces=(), dtype=jnp.bfloat16):
    level = block_scale(rng, dims, pieces, -0.22, 0.18) if pieces else 1.0
    drawn = jax.random.normal(rng, dims, jnp.float32) * deviation * level
    return jnp.minimum(jnp.maximum(drawn, -limit), limit).astype(dtype)


def setup_inputs(seed: int = 0) -> dict:
    keys = jax.random.split(jax.random.key(seed), 6)
    return {
        "factor_t": bell_draw(keys[0], (PANELS, PW, NROW * PW), (NROW * PW // 4) ** -0.5, 0.03125, ((1, 16), (2, 32))),
        "pattern": draw_pattern(jax.random.fold_in(keys[5], 71), 0),
        "diag_inverse": draw_diag_inverse(jax.random.fold_in(keys[5], 71), 0),
        "right_side": bell_draw(keys[3], (NROW * PW, RHS), 1.0, 6.0, ((0, 512),)),
        "later_solution": bell_draw(keys[4], (NROW * PW, RHS), 1.0, 6.0, ((0, 512),)),
    }


def reference(factor_t, pattern, diag_inverse, right_side, later_solution):
    present = jnp.repeat(pattern.T, PW, axis=1).astype(jnp.bfloat16)
    factor = factor_t * present[:, None, :]
    solved_list = []
    for panel_id in range(PANELS):
        first_row = panel_id * RB * PW
        residual = right_side[first_row:first_row + PW].astype(jnp.float32)
        for earlier in range(panel_id):
            residual = residual - jnp.dot(factor[earlier, :, first_row:first_row + PW].T, solved_list[earlier], preferred_element_type=jnp.float32)
        solved_list.append(jnp.dot(diag_inverse[panel_id], residual.astype(jnp.bfloat16), preferred_element_type=jnp.float32).astype(jnp.bfloat16))
    stacked = jnp.stack(solved_list)
    lower = jnp.dot(factor.reshape(PANELS * PW, NROW * PW).T, stacked.reshape(PANELS * PW, RHS), preferred_element_type=jnp.float32)
    reduced = (right_side.astype(jnp.float32) - lower).astype(jnp.bfloat16)
    full = later_solution
    answers = [None] * PANELS
    for panel_id in reversed(range(PANELS)):
        column_total = jnp.dot(factor[panel_id], full, preferred_element_type=jnp.float32)
        gap_value = stacked[panel_id].astype(jnp.float32) - column_total
        solved = jnp.dot(diag_inverse[panel_id].astype(jnp.float32).T, gap_value, precision=lax.Precision.HIGHEST).astype(jnp.bfloat16)
        answers[panel_id] = solved
        first_row = panel_id * RB * PW
        full = full.at[first_row:first_row + PW].set(solved)
    return jnp.stack(answers), reduced
```

```python
import jax
import jax.numpy as jnp
from jax import lax
from jax.experimental import pallas as pl
from jax.experimental.pallas import tpu as pltpu
from jax.sharding import PartitionSpec as P

ROOT = 0
F32 = jnp.float32
BF16 = jnp.bfloat16


def dot(a, b, ca=1, cb=0):
    return lax.dot_general(a, b, (((ca,), (cb,)), ((), ())), preferred_element_type=F32)


def remote(src, dst, send_sem, recv_sem, **device):
    return pltpu.make_async_remote_copy(
        src_ref=src,
        dst_ref=dst,
        send_sem=send_sem,
        recv_sem=recv_sem,
        device_id=device,
        device_id_type=pl.DeviceIdType.MESH,
    )


def signal(sem, **device):
    pl.semaphore_signal(sem, inc=1, device_id=device, device_id_type=pl.DeviceIdType.MESH)


def kernel(rows_n, cols_n, panels, width, *refs):
    factor, pattern, diag, right, later, sol_out, red_out = refs[:7]
    (
        full, inv, lead_own, lead, rt_slabs, rt_own, rt_all, bulk, bulk_in, z_own, z_in,
        y_own, y_all, s_own, s_all, out_buf, right_v, later_v,
    ) = refs[7:25]
    (
        loc, bar_unused, fa, fb, da, db, la, lb, ga, gb, ra, rb, qa, qb, sa, sb, za, zb,
        ya, yb, va, vb, ta, tb, oa, ob,
    ) = refs[25:]
    del bar_unused
    row = lax.axis_index("prow")
    col = lax.axis_index("pcol")
    narrow = width // cols_n
    is_root = row == ROOT

    copies = [
        pltpu.make_async_copy(right, right_v, loc.at[0]),
        pltpu.make_async_copy(later, later_v, loc.at[1]),
    ]
    for copy in copies:
        copy.start()

    barrier = pltpu.get_barrier_semaphore()

    def greet_col(i, _):
        signal(barrier, pcol=lax.rem(col + i, cols_n))
        return 0

    def greet_row(i, _):
        signal(barrier, prow=lax.rem(row + i, rows_n))
        return 0

    lax.fori_loop(1, cols_n, greet_col, 0)

    @pl.when(is_root)
    def _():
        lax.fori_loop(1, rows_n, greet_row, 0)
        pl.semaphore_wait(barrier, cols_n - 1 + rows_n - 1)

    @pl.when(row != ROOT)
    def _():
        signal(barrier, prow=ROOT)
        pl.semaphore_wait(barrier, cols_n)

    def strip(ref, j):
        return ref.at[:, pl.ds(pl.multiple_of(j * narrow, narrow), narrow), :]

    def pcol_each(make, what):
        def step(i, _):
            getattr(make(i, lax.rem(col + i, cols_n)), what)()
            return 0

        lax.fori_loop(1, cols_n, step, 0)

    class Exchange:
        def __init__(self, src, dst, send, recv):
            self.src, self.dst, self.send, self.recv = src, dst, send, recv

        def start(self):
            pcol_each(
                lambda i, j: remote(
                    self.src(j), self.dst(col), self.send.at[i], self.recv.at[col], pcol=j
                ),
                "start",
            )

        def arrive(self):
            pcol_each(
                lambda i, j: remote(
                    self.src(j), self.dst(j), self.send.at[i], self.recv.at[j], pcol=j
                ),
                "wait_recv",
            )

        def drain(self):
            pcol_each(
                lambda i, j: remote(
                    self.src(j), self.dst(j), self.send.at[i], self.recv.at[j], pcol=j
                ),
                "wait_send",
            )

    def factor_block(j):
        return factor.at[:, :, pl.ds(pl.multiple_of(j * width, width), width)]

    factor_x = Exchange(factor_block, lambda j: strip(full, j), fa, fb)
    inv_x = Exchange(lambda j: diag, lambda j: strip(inv, j), da, db)
    lead_x = Exchange(lambda j: lead_own, lambda j: strip(lead, j), ga, gb)
    bulk_x = Exchange(lambda j: bulk.at[j], lambda j: bulk_in.at[j], sa, sb)
    y_x = Exchange(lambda j: y_own, lambda j: y_all.at[j], va, vb)
    sol_x = Exchange(lambda j: s_own, lambda j: s_all.at[j], ta, tb)

    def lead_copy(q):
        first = q * (q - 1) // 2
        return remote(
            factor.at[pl.ds(0, q), :, pl.ds(0, width)],
            lead_own.at[pl.ds(first, q)],
            la,
            lb.at[q],
            prow=ROOT,
        )

    for q in range(1, panels):

        @pl.when(row == q)
        def _(q=q):
            lead_copy(q).start()

    factor_x.start()
    own_factor = pltpu.make_async_copy(factor_block(col), strip(full, col), loc.at[2])
    own_factor.start()

    @pl.when(is_root)
    def _():
        inv_x.start()
        pltpu.make_async_copy(diag, strip(inv, col), loc.at[3]).start()

    for copy in copies:
        copy.wait()

    def rt_scatter(j):
        return remote(rt_slabs.at[j], rt_own, ra.at[j], rb, pcol=j)

    @pl.when((row < panels) & (col == 0))
    def _():
        flipped = right_v[...].astype(F32).T.astype(BF16)
        rt_slabs[...] = flipped.reshape(rt_slabs.shape)

        def step(j, _):
            rt_scatter(j).start()
            return 0

        lax.fori_loop(1, cols_n, step, 0)
        rt_own[...] = rt_slabs[0]

    @pl.when((row < panels) & (col != 0))
    def _():
        rt_scatter(0).wait_recv()

    for q in range(1, panels):

        @pl.when(row == q)
        def _(q=q):
            remote(rt_own, rt_all.at[q], qa, qb.at[q], prow=ROOT).start()

    later_t = later_v[...].astype(F32).T.astype(BF16)

    @pl.when(is_root)
    def _():
        rt_all[0] = rt_own[...]
        for q in range(1, panels):
            lead_copy(q).wait_recv()
        lead_x.start()
        pltpu.make_async_copy(lead_own, strip(lead, col), loc.at[4]).start()

    factor_x.arrive()
    own_factor.wait()
    scales = [pattern[col, p].astype(F32) for p in range(panels)]
    outside = jnp.where((row < panels) & (col == 0), 0.0, 1.0).astype(F32)
    for p in range(panels):
        part = dot(later_t, full[p], 1, 1) * (scales[p] * outside)
        bulk[:, :, p * width : (p + 1) * width] = part.astype(BF16).reshape(
            cols_n, narrow, width
        )
    bulk_x.start()

    def y_send(r):
        return remote(y_own, y_own, ya.at[r], yb, prow=r)

    @pl.when(is_root)
    def _():
        inv_x.arrive()
        pltpu.make_async_copy(diag, strip(inv, col), loc.at[3]).wait()
        lead_x.arrive()
        pltpu.make_async_copy(lead_own, strip(lead, col), loc.at[4]).wait()
        solved = []
        for q in range(panels):
            if q > 0:
                remote(rt_own, rt_all.at[q], qa, qb.at[q], prow=ROOT).wait_recv()
            residual = rt_all[q].astype(F32)
            for p in range(q):
                residual = residual - dot(solved[p], lead[q * (q - 1) // 2 + p])
            y_p = dot(residual.astype(BF16), inv[q], 1, 1).astype(BF16)
            solved.append(y_p)
            y_own[:, q * width : (q + 1) * width] = y_p

        def step(r, _):
            y_send(r).start()
            return 0

        lax.fori_loop(1, rows_n, step, 0)
        y_x.start()

    bulk_x.arrive()
    total = bulk[col].astype(F32)
    for i in range(1, cols_n):
        total = total + bulk_in[lax.rem(col + i, cols_n)].astype(F32)

    def z_send(r):
        return remote(z_own, z_in.at[r], za, zb.at[r], prow=ROOT)

    @pl.when(row != ROOT)
    def _():
        z_own[...] = total.astype(BF16)
        z_send(row).start()
        y_send(0).wait_recv()
        y_x.start()

    def out_send(r):
        return remote(out_buf, out_buf, oa.at[r], ob, prow=r)

    @pl.when(is_root)
    def _():
        gathered = total
        for r in range(1, rows_n):
            z_send(r).wait_recv()
            gathered = gathered + z_in[r].astype(F32)
        answers = [None] * panels
        for p in reversed(range(panels)):
            column = gathered[:, p * width : (p + 1) * width]
            for q in range(panels - 1, p, -1):
                column = column + dot(answers[q], lead[q * (q - 1) // 2 + p], 1, 1)
            gap = y_own[:, p * width : (p + 1) * width].astype(F32) - column
            high = gap.astype(BF16)
            rest = gap - high.astype(F32)
            middle = rest.astype(BF16)
            low = (rest - middle.astype(F32)).astype(BF16)
            applied = dot(high, inv[p]) + (dot(middle, inv[p]) + dot(low, inv[p]))
            answers[p] = applied.astype(BF16)
            s_own[:, p * width : (p + 1) * width] = answers[p]
        sol_x.start()
        s_all[col] = s_own[...]
        sol_x.arrive()
        mine = lax.broadcasted_iota(jnp.int32, (narrow, width), 0) + col * narrow
        pick = (lax.broadcasted_iota(jnp.int32, (narrow, width), 1) == mine).astype(BF16)
        for p in range(panels):
            block = s_all[:, :, p * width : (p + 1) * width].reshape(-1, width)
            out_buf[p] = dot(pick, block, 1, 1).astype(BF16)

        def step(r, _):
            out_send(r).start()
            return 0

        lax.fori_loop(1, rows_n, step, 0)
        sol_out[...] = out_buf[...]

    y_all[col] = y_own[...]
    y_x.arrive()
    lower_t = jnp.zeros((width, width), F32)
    for p in range(panels):
        y_p = y_all[:, :, p * width : (p + 1) * width].reshape(-1, width)
        lower_t = lower_t + dot(y_p, full[p]) * scales[p]
    red_out[...] = (right_v[...].astype(F32) - lower_t.T).astype(BF16)

    @pl.when(row != ROOT)
    def _():
        out_send(0).wait_recv()
        sol_out[...] = out_buf[...]

    factor_x.drain()
    bulk_x.drain()
    y_x.drain()

    @pl.when((row < panels) & (col == 0))
    def _():
        def step(j, _):
            rt_scatter(j).wait_send()
            return 0

        lax.fori_loop(1, cols_n, step, 0)

    for q in range(1, panels):

        @pl.when(row == q)
        def _(q=q):
            lead_copy(q).wait_send()
            remote(rt_own, rt_all.at[q], qa, qb.at[q], prow=ROOT).wait_send()

    @pl.when(row != ROOT)
    def _():
        z_send(row).wait_send()

    @pl.when(is_root)
    def _():
        inv_x.drain()
        lead_x.drain()
        sol_x.drain()

        def step(r, _):
            y_send(r).wait_send()
            out_send(r).wait_send()
            return 0

        lax.fori_loop(1, rows_n, step, 0)


def solution(mesh):
    rows_n, cols_n = mesh.shape["prow"], mesh.shape["pcol"]

    def on_device(factor_t, pattern, diag_inverse, right_side, later_solution):
        panels, narrow, _ = factor_t.shape
        width = diag_inverse.shape[2]
        rhs = right_side.shape[1]
        pairs = panels * (panels - 1) // 2
        slab = (rhs // cols_n, panels * width)
        dma = pltpu.SemaphoreType.DMA
        per_col, per_row = dma((cols_n,)), dma((rows_n,))
        vmem = pltpu.VMEM
        scratch = [
            vmem((panels, width, width), BF16),
            vmem((panels, width, width), BF16),
            vmem((pairs, narrow, width), BF16),
            vmem((pairs, width, width), BF16),
            vmem((cols_n, rhs // cols_n, width), BF16),
            vmem((rhs // cols_n, width), BF16),
            vmem((panels, rhs // cols_n, width), BF16),
            vmem((cols_n,) + slab, BF16),
            vmem((cols_n,) + slab, BF16),
            vmem(slab, BF16),
            vmem((rows_n,) + slab, BF16),
            vmem(slab, BF16),
            vmem((cols_n,) + slab, BF16),
            vmem(slab, BF16),
            vmem((cols_n,) + slab, BF16),
            vmem((panels, narrow, rhs), BF16),
            vmem(right_side.shape, BF16),
            vmem(later_solution.shape, BF16),
            dma((8,)),
            dma,
            per_col, per_col,
            per_col, per_col,
            dma, dma((panels,)),
            per_col, per_col,
            per_col, dma,
            dma, dma((panels,)),
            per_col, per_col,
            dma, per_row,
            per_row, dma,
            per_col, per_col,
            per_col, per_col,
            per_row, dma,
        ]
        anywhere = pl.BlockSpec(memory_space=pl.ANY)
        return pl.pallas_call(
            lambda *refs: kernel(rows_n, cols_n, panels, width, *refs),
            out_shape=(
                jax.ShapeDtypeStruct((panels, narrow, rhs), BF16),
                jax.ShapeDtypeStruct(right_side.shape, BF16),
            ),
            in_specs=[
                anywhere,
                pl.BlockSpec(memory_space=pltpu.SMEM),
                anywhere,
                anywhere,
                anywhere,
            ],
            out_specs=(
                pl.BlockSpec(memory_space=pltpu.VMEM),
                pl.BlockSpec(memory_space=pltpu.VMEM),
            ),
            scratch_shapes=scratch,
            compiler_params=pltpu.CompilerParams(
                collective_id=0, has_side_effects=True, vmem_limit_bytes=48 << 20
            ),
            name="solve",
        )(factor_t, pattern, diag_inverse, right_side, later_solution)

    in_specs = (
        P(None, "pcol", "prow"),
        P("prow", None),
        P(None, "pcol", None),
        P(("prow", "pcol"), None),
        P(("prow", "pcol"), None),
    )
    out_specs = (P(None, "pcol", None), P(("prow", "pcol"), None))
    return jax.shard_map(
        on_device, mesh=mesh, in_specs=in_specs, out_specs=out_specs, check_vma=False
    )
```

```python
import math

import jax
import jax.numpy as jnp
from jax import lax
from jax.experimental import pallas as pl
from jax.experimental.pallas import tpu as pltpu
from jax.sharding import PartitionSpec as P

ROOT = 0
F32 = jnp.float32
BF16 = jnp.bfloat16


def dot(a, b, ca=1, cb=0):
    return lax.dot_general(a, b, (((ca,), (cb,)), ((), ())), preferred_element_type=F32)


def remote(src, dst, send_sem, recv_sem, **device):
    return pltpu.make_async_remote_copy(
        src_ref=src,
        dst_ref=dst,
        send_sem=send_sem,
        recv_sem=recv_sem,
        device_id=device,
        device_id_type=pl.DeviceIdType.MESH,
    )


def signal(sem, **device):
    pl.semaphore_signal(sem, inc=1, device_id=device, device_id_type=pl.DeviceIdType.MESH)


def kernel(rows_n, cols_n, panels, width, *refs):
    factor, pattern, diag, right, later, sol_out, red_out = refs[:7]
    (
        part, later_all, inv, lead_own, lead, rt_slabs, rt_own, rt_all, bulk, bulk_in, z_own,
        z_in, y_own, y_keep, y_all, low, low_in, spread, sol_in, out_buf, right_v, acc,
    ) = refs[7:29]
    (
        loc, hello, fa, fb, ha, hb, da, db, la, lb, ga, gb, ra, rb, qa, qb, sa, sb, za, zb,
        ya, yb, va, vb, wa, wb, ta, tb, oa, ob,
    ) = refs[29:]
    row = lax.axis_index("prow")
    col = lax.axis_index("pcol")
    side = math.isqrt(cols_n)
    x, y = lax.div(col, side), lax.rem(col, side)
    narrow = width // cols_n
    group = side * narrow
    quarter = side * width
    is_root = row == ROOT

    fetch = pltpu.make_async_copy(right, right_v, loc.at[0])
    fetch.start()

    barrier = pltpu.get_barrier_semaphore()

    def greet_col(i, _):
        signal(barrier, pcol=lax.rem(col + i, cols_n))
        return 0

    def greet_row(i, _):
        signal(barrier, prow=lax.rem(row + i, rows_n))
        return 0

    lax.fori_loop(1, cols_n, greet_col, 0)
    @pl.when(is_root)
    def _():
        lax.fori_loop(1, rows_n, greet_row, 0)

    @pl.when(lax.rem(row, 2) == 1)
    def _():
        signal(barrier, prow=row - 1)

    expected = cols_n - 1 + jnp.where(is_root, 0, 1) + (1 - lax.rem(row, 2))
    pl.semaphore_wait(barrier, expected)

    def strip(ref, j):
        return ref.at[:, pl.ds(pl.multiple_of(j * narrow, narrow), narrow), :]

    class Exchange:
        def __init__(self, count, peer, src, dst, send, recv, me):
            self.count, self.peer, self.src, self.dst = count, peer, src, dst
            self.send, self.recv, self.me = send, recv, me

        def each(self, what):
            def step(i, _):
                device, j = self.peer(i)
                to = self.me if what == "start" else j
                getattr(
                    remote(
                        self.src(j), self.dst(to), self.send.at[i], self.recv.at[to], pcol=device
                    ),
                    what,
                )()
                return 0

            lax.fori_loop(1, self.count, step, 0)

        def start(self):
            self.each("start")

        def arrive(self):
            self.each("wait_recv")

        def drain(self):
            self.each("wait_send")

    def any_peer(i):
        j = lax.rem(col + i, cols_n)
        return j, j

    def x_peer(i):
        j = lax.rem(x + i, side)
        return j * side + y, j

    def y_peer(i):
        j = lax.rem(y + i, side)
        return x * side + j, j

    def over_all(src, dst, send, recv):
        return Exchange(cols_n, any_peer, src, dst, send, recv, col)

    def turned(j):
        return lax.rem(j, side) * side + lax.div(j, side)

    def factor_quarter(j):
        return factor.at[:, :, pl.ds(pl.multiple_of(j * quarter, quarter), quarter)]

    def later_strip(j):
        return later_all.at[pl.ds(pl.multiple_of(j * width, width), width), :]

    factor_x = Exchange(
        side, x_peer, factor_quarter, lambda j: strip(part, j), fa, fb, x
    )
    later_x = Exchange(side, y_peer, lambda j: later, later_strip, ha, hb, y)
    inv_x = over_all(lambda j: diag, lambda j: strip(inv, turned(j)), da, db)
    lead_x = over_all(lambda j: lead_own, lambda j: strip(lead, turned(j)), ga, gb)
    bulk_x = over_all(lambda j: bulk.at[j], lambda j: bulk_in.at[j], sa, sb)
    y_x = over_all(lambda j: y_own.at[lax.rem(j, side)], lambda j: y_all.at[j], va, vb)
    low_x = Exchange(
        side, y_peer, lambda j: low.at[j], lambda j: low_in.at[j], wa, wb, y
    )
    sol_x = over_all(lambda j: strip(spread, j), lambda j: sol_in.at[j], ta, tb)

    factor_x.start()
    later_x.start()
    own_copies = [
        pltpu.make_async_copy(factor_quarter(x), strip(part, x), loc.at[1]),
        pltpu.make_async_copy(later, later_strip(y), loc.at[2]),
    ]
    for copy in own_copies:
        copy.start()

    @pl.when(row != ROOT)
    def _():
        signal(hello, prow=ROOT)

    def lead_copy(q):
        first = q * (q - 1) // 2
        return remote(
            factor.at[pl.ds(0, q), :, pl.ds(0, width)],
            lead_own.at[pl.ds(first, q)],
            la,
            lb.at[q],
            prow=ROOT,
        )

    for q in range(1, panels):

        @pl.when(row == q)
        def _(q=q):
            lead_copy(q).start()

    @pl.when(is_root)
    def _():
        inv_x.start()
        pltpu.make_async_copy(diag, strip(inv, turned(col)), loc.at[3]).start()

    fetch.wait()

    def rt_scatter(j):
        return remote(rt_slabs.at[j], rt_own, ra.at[j], rb, pcol=j)

    @pl.when((row < panels) & (col == 0))
    def _():
        flipped = right_v[...].astype(F32).T.astype(BF16)
        rt_slabs[...] = flipped.reshape(rt_slabs.shape)

        def step(j, _):
            rt_scatter(j).start()
            return 0

        lax.fori_loop(1, cols_n, step, 0)
        rt_own[...] = rt_slabs[0]

    @pl.when((row < panels) & (col != 0))
    def _():
        rt_scatter(0).wait_recv()

    def rt_send(q):
        return remote(rt_own, rt_all.at[q], qa, qb.at[q], prow=ROOT)

    for q in range(1, panels):

        @pl.when(row == q)
        def _(q=q):
            rt_send(q).start()

    @pl.when(is_root)
    def _():
        rt_all[0] = rt_own[...]
        for q in range(1, panels):
            lead_copy(q).wait_recv()
        lead_x.start()
        pltpu.make_async_copy(lead_own, strip(lead, turned(col)), loc.at[4]).start()

    factor_x.arrive()
    later_x.arrive()
    for copy in own_copies:
        copy.wait()
    columns = panels * group

    @pl.when((row < panels) & (x == 0))
    def _():
        later_all[:width, :] = jnp.zeros((width, later_all.shape[1]), BF16)

    acc[...] = jnp.zeros_like(acc)

    def block_of(b):
        return pl.ds(pl.multiple_of(b * width, width), width)

    def bulk_step(b, _):
        rows = block_of(b)
        pieces = []
        for p in range(panels):
            keep = pattern[p, x * side + b].astype(F32).astype(BF16)
            piece = part[p, :, rows] * keep
            part[p, :, rows] = piece
            pieces.append(piece)
        acc[...] += dot(jnp.concatenate(pieces, axis=0), later_all[rows, :])
        return 0

    lax.fori_loop(0, side, bulk_step, 0)
    bulk[...] = acc[...].T.astype(BF16).reshape(bulk.shape)
    bulk_x.start()
    bulk_in[col] = bulk[col]

    chips = rows_n // 2

    def along_row(send):
        def step(i, _):
            send(2 * i).start()
            return 0

        lax.fori_loop(1, chips, step, 0)
        send(1).start()

    first_core = lax.rem(row, 2) == 0
    relays = first_core & (row != ROOT)

    def y_send(r):
        return remote(y_own, y_own, ya.at[r], yb, prow=r)

    @pl.when(is_root)
    def _():
        inv_x.arrive()
        pltpu.make_async_copy(diag, strip(inv, turned(col)), loc.at[3]).wait()
        lead_x.arrive()
        pltpu.make_async_copy(lead_own, strip(lead, turned(col)), loc.at[4]).wait()
        solved = []
        for q in range(panels):
            if q > 0:
                rt_send(q).wait_recv()
            residual = rt_all[q].astype(F32)
            for p in range(q):
                residual = residual - dot(solved[p], lead[q * (q - 1) // 2 + p])
            y_q = dot(residual.astype(BF16), inv[q], 1, 1).astype(BF16)
            solved.append(y_q)
            y_keep[q] = y_q
        for j in range(side):
            pieces = [y_q[:, j * group : (j + 1) * group] for y_q in solved]
            y_own[j] = jnp.concatenate(pieces, axis=1)
        pl.semaphore_wait(hello, rows_n - 1)

        along_row(y_send)
        y_x.start()

    bulk_x.arrive()
    def sum_step(i, sums):
        return tuple(t + bulk_in[i * side + j].astype(F32) for j, t in enumerate(sums))

    sums = lax.fori_loop(
        1, side, sum_step, tuple(bulk_in[j].astype(F32) for j in range(side))
    )
    for p in range(panels):
        pieces = [total[:, p * group : (p + 1) * group] for total in sums]
        z_own[p] = jnp.concatenate(pieces, axis=1).astype(z_own.dtype)

    def z_send(r):
        return remote(z_own, z_in.at[r], za, zb.at[r], prow=ROOT)

    @pl.when(row != ROOT)
    def _():
        z_send(row).start()
        y_send(0).wait_recv()

        @pl.when(relays)
        def _():
            y_send(row + 1).start()

        y_x.start()

    def out_send(r):
        return remote(out_buf, out_buf, oa.at[r], ob, prow=r)

    @pl.when(is_root)
    def _():
        def gather_step(r, sums):
            z_send(r).wait_recv()
            return tuple(t + z_in[r, p].astype(F32) for p, t in enumerate(sums))

        gathered = lax.fori_loop(
            1, rows_n, gather_step, tuple(z_own[p].astype(F32) for p in range(panels))
        )
        answers = [None] * panels
        shift = lax.rem(col, cols_n // 2) * narrow
        shape = (narrow, 128)
        at = lax.broadcasted_iota(jnp.int32, shape, 0) + shift
        place = (lax.broadcasted_iota(jnp.int32, shape, 1) == at).astype(BF16)
        for p in reversed(range(panels)):
            column = gathered[p]
            for q in range(panels - 1, p, -1):
                column = column + dot(answers[q], lead[q * (q - 1) // 2 + p], 1, 1)
            gap = y_keep[p].astype(F32) - column
            high = gap.astype(BF16)
            rest = gap - high.astype(F32)
            middle = rest.astype(BF16)
            lowest = (rest - middle.astype(F32)).astype(BF16)
            parts = dot(jnp.concatenate([high, middle, lowest], axis=0), inv[p])
            applied = parts[:narrow] + (parts[narrow : 2 * narrow] + parts[2 * narrow :])
            answers[p] = applied.astype(BF16)
            spread[p] = dot(answers[p], place, 0, 0).astype(BF16)
        sol_x.start()
        mine = pl.ds(pl.multiple_of(col * narrow, narrow), narrow)
        sol_in[col] = spread[:, mine, :]

    y_all[col] = y_own[y]
    y_x.arrive()

    def lower_step(j, _):
        strip_j = part[:, :, block_of(j)].reshape(columns, width)
        low[j] = dot(y_all[...].reshape(-1, columns), strip_j).astype(BF16)
        return 0

    lax.fori_loop(0, side, lower_step, 0)
    low_x.start()
    low_in[y] = low[y]

    @pl.when(is_root)
    def _():
        sol_x.arrive()
        half = cols_n // 2

        def merge_step(j, sums):
            first, second = sums
            return first + sol_in[j].astype(F32), second + sol_in[half + j].astype(F32)

        merged = lax.fori_loop(
            1, half, merge_step, (sol_in[0].astype(F32), sol_in[half].astype(F32))
        )
        out_buf[:, :, :128] = merged[0].astype(BF16)
        out_buf[:, :, 128:] = merged[1].astype(BF16)

        along_row(out_send)

    low_x.arrive()
    lower_t = low_in[0].astype(F32)
    for j in range(1, side):
        lower_t = lower_t + low_in[j].astype(F32)
    red_out[...] = (right_v[...].astype(F32) - lower_t.T).astype(BF16)

    @pl.when(row != ROOT)
    def _():
        out_send(0).wait_recv()

        @pl.when(relays)
        def _():
            out_send(row + 1).start()

    sol_out[...] = out_buf[...]

    for exchange in (factor_x, later_x, bulk_x, y_x, low_x):
        exchange.drain()

    @pl.when((row < panels) & (col == 0))
    def _():
        def step(j, _):
            rt_scatter(j).wait_send()
            return 0

        lax.fori_loop(1, cols_n, step, 0)

    for q in range(1, panels):

        @pl.when(row == q)
        def _(q=q):
            lead_copy(q).wait_send()
            rt_send(q).wait_send()

    @pl.when(row != ROOT)
    def _():
        z_send(row).wait_send()

    @pl.when(is_root)
    def _():
        inv_x.drain()
        lead_x.drain()
        sol_x.drain()

        def step(i, _):
            y_send(2 * i).wait_send()
            out_send(2 * i).wait_send()
            return 0

        lax.fori_loop(1, chips, step, 0)

    @pl.when(first_core)
    def _():
        y_send(row + 1).wait_send()
        out_send(row + 1).wait_send()


def solution(mesh):
    rows_n, cols_n = mesh.shape["prow"], mesh.shape["pcol"]

    def on_device(factor_t, pattern, diag_inverse, right_side, later_solution):
        panels, narrow, _ = factor_t.shape
        width = diag_inverse.shape[2]
        rhs = right_side.shape[1]
        pairs = panels * (panels - 1) // 2
        side = math.isqrt(cols_n)
        group, quarter = side * narrow, side * width
        own = rhs // cols_n
        dma = pltpu.SemaphoreType.DMA
        per_col, per_row, per_side = dma((cols_n,)), dma((rows_n,)), dma((side,))
        vmem = pltpu.VMEM
        scratch = [
            vmem((panels, group, quarter), BF16),
            vmem((quarter, rhs), BF16),
            vmem((panels, width, width), BF16),
            vmem((pairs, narrow, width), BF16),
            vmem((pairs, width, width), BF16),
            vmem((cols_n, own, width), BF16),
            vmem((own, width), BF16),
            vmem((panels, own, width), BF16),
            vmem((cols_n, own, panels * group), BF16),
            vmem((cols_n, own, panels * group), BF16),
            vmem((panels, own, width), BF16),
            vmem((rows_n, panels, own, width), BF16),
            vmem((side, own, panels * group), BF16),
            vmem((panels, own, width), BF16),
            vmem((cols_n, own, panels * group), BF16),
            vmem((side, rhs, width), BF16),
            vmem((side, rhs, width), BF16),
            vmem((panels, width, 128), BF16),
            vmem((cols_n, panels, narrow, 128), BF16),
            vmem((panels, narrow, rhs), BF16),
            vmem(right_side.shape, BF16),
            vmem((panels * group, rhs), F32),
            dma((8,)),
            pltpu.SemaphoreType.REGULAR,
            per_side, per_side,
            per_side, per_side,
            per_col, per_col,
            dma, dma((panels,)),
            per_col, per_col,
            per_col, dma,
            dma, dma((panels,)),
            per_col, per_col,
            dma, per_row,
            per_row, dma,
            per_col, per_col,
            per_side, per_side,
            per_col, per_col,
            per_row, dma,
        ]
        anywhere = pl.BlockSpec(memory_space=pl.ANY)
        return pl.pallas_call(
            lambda *refs: kernel(rows_n, cols_n, panels, width, *refs),
            out_shape=(
                jax.ShapeDtypeStruct((panels, narrow, rhs), BF16),
                jax.ShapeDtypeStruct(right_side.shape, BF16),
            ),
            in_specs=[
                anywhere,
                pl.BlockSpec(memory_space=pltpu.SMEM),
                anywhere,
                anywhere,
                anywhere,
            ],
            out_specs=(
                pl.BlockSpec(memory_space=pltpu.VMEM),
                pl.BlockSpec(memory_space=pltpu.VMEM),
            ),
            scratch_shapes=scratch,
            compiler_params=pltpu.CompilerParams(
                collective_id=0, has_side_effects=True, vmem_limit_bytes=62 << 20
            ),
            name="solve",
        )(factor_t, pattern.T, diag_inverse, right_side, later_solution)

    in_specs = (
        P(None, "pcol", "prow"),
        P("prow", None),
        P(None, "pcol", None),
        P(("prow", "pcol"), None),
        P(("prow", "pcol"), None),
    )
    out_specs = (P(None, "pcol", None), P(("prow", "pcol"), None))
    return jax.shard_map(
        on_device, mesh=mesh, in_specs=in_specs, out_specs=out_specs, check_vma=False
    )
```

```python
import math

import jax
import jax.numpy as jnp
from jax import lax
from jax.experimental import pallas as pl
from jax.experimental.pallas import tpu as pltpu
from jax.sharding import PartitionSpec as P

ROOT = 0
F32 = jnp.float32
BF16 = jnp.bfloat16


def dot(a, b, ca=1, cb=0):
    return lax.dot_general(a, b, (((ca,), (cb,)), ((), ())), preferred_element_type=F32)


def remote(src, dst, send_sem, recv_sem, **device):
    return pltpu.make_async_remote_copy(
        src_ref=src,
        dst_ref=dst,
        send_sem=send_sem,
        recv_sem=recv_sem,
        device_id=device,
        device_id_type=pl.DeviceIdType.MESH,
    )


def signal(sem, **device):
    pl.semaphore_signal(sem, inc=1, device_id=device, device_id_type=pl.DeviceIdType.MESH)


def kernel(rows_n, cols_n, panels, width, *refs):
    factor, pattern_in, diag, right, later, sol_out, red_out = refs[:7]
    (
        part, later_all, inv, lead_own, lead, rt_slabs, rt_own, rt_all, bulk, bulk_in, z_own,
        z_in, y_own, y_keep, y_all, low, low_in, spread, sol_in, out_buf, right_v, acc, pattern,
    ) = refs[7:30]
    (
        loc, hello, fa, fb, ha, hb, da, db, la, lb, ga, gb, ra, rb, qa, qb, sa, sb, za, zb,
        ya, yb, va, vb, wa, wb, ta, tb, oa, ob,
    ) = refs[30:]
    row = lax.axis_index("prow")
    col = lax.axis_index("pcol")
    side = math.isqrt(cols_n)
    x, y = lax.div(col, side), lax.rem(col, side)
    narrow = width // cols_n
    group = side * narrow
    quarter = side * width
    is_root = row == ROOT

    fetch = pltpu.make_async_copy(right, right_v, loc.at[0])
    fetch.start()
    fetch_pattern = pltpu.make_async_copy(pattern_in, pattern, loc.at[5])
    fetch_pattern.start()

    barrier = pltpu.get_barrier_semaphore()

    def greet_col(i, _):
        signal(barrier, pcol=lax.rem(col + i, cols_n))
        return 0

    def greet_row(i, _):
        signal(barrier, prow=lax.rem(row + i, rows_n))
        return 0

    lax.fori_loop(1, cols_n, greet_col, 0)
    @pl.when(is_root)
    def _():
        lax.fori_loop(1, rows_n, greet_row, 0)

    @pl.when(lax.rem(row, 2) == 1)
    def _():
        signal(barrier, prow=row - 1)

    expected = cols_n - 1 + jnp.where(is_root, 0, 1) + (1 - lax.rem(row, 2))
    pl.semaphore_wait(barrier, expected)

    def strip(ref, j):
        return ref.at[:, pl.ds(pl.multiple_of(j * narrow, narrow), narrow), :]

    class Exchange:
        def __init__(self, count, peer, src, dst, send, recv, me):
            self.count, self.peer, self.src, self.dst = count, peer, src, dst
            self.send, self.recv, self.me = send, recv, me

        def each(self, what):
            def step(i, _):
                device, j = self.peer(i)
                to = self.me if what == "start" else j
                getattr(
                    remote(
                        self.src(j), self.dst(to), self.send.at[i], self.recv.at[to], pcol=device
                    ),
                    what,
                )()
                return 0

            lax.fori_loop(1, self.count, step, 0)

        def start(self):
            self.each("start")

        def arrive(self):
            self.each("wait_recv")

        def drain(self):
            self.each("wait_send")

    def any_peer(i):
        j = lax.rem(col + i, cols_n)
        return j, j

    def x_peer(i):
        j = lax.rem(x + i, side)
        return j * side + y, j

    def y_peer(i):
        j = lax.rem(y + i, side)
        return x * side + j, j

    def over_all(src, dst, send, recv):
        return Exchange(cols_n, any_peer, src, dst, send, recv, col)

    def turned(j):
        return lax.rem(j, side) * side + lax.div(j, side)

    def factor_quarter(j):
        return factor.at[:, :, pl.ds(pl.multiple_of(j * quarter, quarter), quarter)]

    def later_strip(j):
        return later_all.at[pl.ds(pl.multiple_of(j * width, width), width), :]

    factor_x = Exchange(
        side, x_peer, factor_quarter, lambda j: strip(part, j), fa, fb, x
    )
    later_x = Exchange(side, y_peer, lambda j: later, later_strip, ha, hb, y)
    inv_x = over_all(lambda j: diag, lambda j: strip(inv, turned(j)), da, db)
    lead_x = over_all(lambda j: lead_own, lambda j: strip(lead, turned(j)), ga, gb)
    bulk_x = over_all(lambda j: bulk.at[j], lambda j: bulk_in.at[j], sa, sb)
    y_x = over_all(lambda j: y_own.at[lax.rem(j, side)], lambda j: y_all.at[j], va, vb)
    low_x = Exchange(
        side, y_peer, lambda j: low.at[j], lambda j: low_in.at[j], wa, wb, y
    )
    sol_x = over_all(lambda j: strip(spread, j), lambda j: sol_in.at[j], ta, tb)

    factor_x.start()
    later_x.start()
    own_copies = [
        pltpu.make_async_copy(factor_quarter(x), strip(part, x), loc.at[1]),
        pltpu.make_async_copy(later, later_strip(y), loc.at[2]),
    ]
    for copy in own_copies:
        copy.start()

    @pl.when(row != ROOT)
    def _():
        signal(hello, prow=ROOT)

    def lead_copy(q):
        first = q * (q - 1) // 2
        return remote(
            factor.at[pl.ds(0, q), :, pl.ds(0, width)],
            lead_own.at[pl.ds(first, q)],
            la,
            lb.at[q],
            prow=ROOT,
        )

    for q in range(1, panels):

        @pl.when(row == q)
        def _(q=q):
            lead_copy(q).start()

    @pl.when(is_root)
    def _():
        inv_x.start()
        pltpu.make_async_copy(diag, strip(inv, turned(col)), loc.at[3]).start()

    fetch.wait()
    fetch_pattern.wait()

    def rt_scatter(j):
        return remote(rt_slabs.at[j], rt_own, ra.at[j], rb, pcol=j)

    @pl.when((row < panels) & (col == 0))
    def _():
        flipped = right_v[...].astype(F32).T.astype(BF16)
        rt_slabs[...] = flipped.reshape(rt_slabs.shape)

        def step(j, _):
            rt_scatter(j).start()
            return 0

        lax.fori_loop(1, cols_n, step, 0)
        rt_own[...] = rt_slabs[0]

    @pl.when((row < panels) & (col != 0))
    def _():
        rt_scatter(0).wait_recv()

    def rt_send(q):
        return remote(rt_own, rt_all.at[q], qa, qb.at[q], prow=ROOT)

    for q in range(1, panels):

        @pl.when(row == q)
        def _(q=q):
            rt_send(q).start()

    @pl.when(is_root)
    def _():
        rt_all[0] = rt_own[...]
        for q in range(1, panels):
            lead_copy(q).wait_recv()
        lead_x.start()
        pltpu.make_async_copy(lead_own, strip(lead, turned(col)), loc.at[4]).start()

    factor_x.arrive()
    later_x.arrive()
    for copy in own_copies:
        copy.wait()
    columns = panels * group

    @pl.when((row < panels) & (x == 0))
    def _():
        later_all[:width, :] = jnp.zeros((width, later_all.shape[1]), BF16)

    acc[...] = jnp.zeros_like(acc)

    def block_of(b):
        return pl.ds(pl.multiple_of(b * width, width), width)

    def bulk_step(b, _):
        rows = block_of(b)
        pieces = []
        for p in range(panels):
            keep = pattern[p, x * side + b].astype(F32).astype(BF16)
            piece = part[p, :, rows] * keep
            part[p, :, rows] = piece
            pieces.append(piece)
        acc[...] += dot(jnp.concatenate(pieces, axis=0), later_all[rows, :])
        return 0

    lax.fori_loop(0, side, bulk_step, 0)
    bulk[...] = acc[...].T.astype(BF16).reshape(bulk.shape)
    bulk_x.start()
    bulk_in[col] = bulk[col]

    chips = rows_n // 2

    def along_row(send):
        def step(i, _):
            send(2 * i).start()
            return 0

        lax.fori_loop(1, chips, step, 0)
        send(1).start()

    first_core = lax.rem(row, 2) == 0
    relays = first_core & (row != ROOT)

    def y_send(r):
        return remote(y_own, y_own, ya.at[r], yb, prow=r)

    @pl.when(is_root)
    def _():
        inv_x.arrive()
        pltpu.make_async_copy(diag, strip(inv, turned(col)), loc.at[3]).wait()
        lead_x.arrive()
        pltpu.make_async_copy(lead_own, strip(lead, turned(col)), loc.at[4]).wait()
        solved = []
        for q in range(panels):
            if q > 0:
                rt_send(q).wait_recv()
            residual = rt_all[q].astype(F32)
            for p in range(q):
                residual = residual - dot(solved[p], lead[q * (q - 1) // 2 + p])
            y_q = dot(residual.astype(BF16), inv[q], 1, 1).astype(BF16)
            solved.append(y_q)
            y_keep[q] = y_q
        for j in range(side):
            pieces = [y_q[:, j * group : (j + 1) * group] for y_q in solved]
            y_own[j] = jnp.concatenate(pieces, axis=1)
        pl.semaphore_wait(hello, rows_n - 1)

        along_row(y_send)
        y_x.start()

    bulk_x.arrive()
    def sum_step(i, sums):
        return tuple(t + bulk_in[i * side + j].astype(F32) for j, t in enumerate(sums))

    sums = lax.fori_loop(
        1, side, sum_step, tuple(bulk_in[j].astype(F32) for j in range(side))
    )
    for p in range(panels):
        pieces = [total[:, p * group : (p + 1) * group] for total in sums]
        z_own[p] = jnp.concatenate(pieces, axis=1).astype(z_own.dtype)

    def z_send(r):
        return remote(z_own, z_in.at[r], za, zb.at[r], prow=ROOT)

    @pl.when(row != ROOT)
    def _():
        z_send(row).start()
        y_send(0).wait_recv()

        @pl.when(relays)
        def _():
            y_send(row + 1).start()

        y_x.start()

    def out_send(r):
        return remote(out_buf, out_buf, oa.at[r], ob, prow=r)

    @pl.when(is_root)
    def _():
        def gather_step(r, sums):
            z_send(r).wait_recv()
            return tuple(t + z_in[r, p].astype(F32) for p, t in enumerate(sums))

        gathered = lax.fori_loop(
            1, rows_n, gather_step, tuple(z_own[p].astype(F32) for p in range(panels))
        )
        answers = [None] * panels
        shift = lax.rem(col, cols_n // 2) * narrow
        shape = (narrow, 128)
        at = lax.broadcasted_iota(jnp.int32, shape, 0) + shift
        place = (lax.broadcasted_iota(jnp.int32, shape, 1) == at).astype(BF16)
        for p in reversed(range(panels)):
            column = gathered[p]
            for q in range(panels - 1, p, -1):
                column = column + dot(answers[q], lead[q * (q - 1) // 2 + p], 1, 1)
            gap = y_keep[p].astype(F32) - column
            high = gap.astype(BF16)
            rest = gap - high.astype(F32)
            middle = rest.astype(BF16)
            lowest = (rest - middle.astype(F32)).astype(BF16)
            parts = dot(jnp.concatenate([high, middle, lowest], axis=0), inv[p])
            applied = parts[:narrow] + (parts[narrow : 2 * narrow] + parts[2 * narrow :])
            answers[p] = applied.astype(BF16)
            spread[p] = dot(answers[p], place, 0, 0).astype(BF16)
        sol_x.start()
        mine = pl.ds(pl.multiple_of(col * narrow, narrow), narrow)
        sol_in[col] = spread[:, mine, :]

    y_all[col] = y_own[y]
    y_x.arrive()

    def lower_step(j, _):
        strip_j = part[:, :, block_of(j)].reshape(columns, width)
        low[j] = dot(y_all[...].reshape(-1, columns), strip_j).astype(BF16)
        return 0

    lax.fori_loop(0, side, lower_step, 0)
    low_x.start()
    low_in[y] = low[y]

    @pl.when(is_root)
    def _():
        sol_x.arrive()
        half = cols_n // 2

        def merge_step(j, sums):
            first, second = sums
            return first + sol_in[j].astype(F32), second + sol_in[half + j].astype(F32)

        merged = lax.fori_loop(
            1, half, merge_step, (sol_in[0].astype(F32), sol_in[half].astype(F32))
        )
        out_buf[:, :, :128] = merged[0].astype(BF16)
        out_buf[:, :, 128:] = merged[1].astype(BF16)

        along_row(out_send)

    low_x.arrive()
    lower_t = low_in[0].astype(F32)
    for j in range(1, side):
        lower_t = lower_t + low_in[j].astype(F32)
    red_out[...] = (right_v[...].astype(F32) - lower_t.T).astype(BF16)

    @pl.when(row != ROOT)
    def _():
        out_send(0).wait_recv()

        @pl.when(relays)
        def _():
            out_send(row + 1).start()

    sol_out[...] = out_buf[...]

    for exchange in (factor_x, later_x, bulk_x, y_x, low_x):
        exchange.drain()

    @pl.when((row < panels) & (col == 0))
    def _():
        def step(j, _):
            rt_scatter(j).wait_send()
            return 0

        lax.fori_loop(1, cols_n, step, 0)

    for q in range(1, panels):

        @pl.when(row == q)
        def _(q=q):
            lead_copy(q).wait_send()
            rt_send(q).wait_send()

    @pl.when(row != ROOT)
    def _():
        z_send(row).wait_send()

    @pl.when(is_root)
    def _():
        inv_x.drain()
        lead_x.drain()
        sol_x.drain()

        def step(i, _):
            y_send(2 * i).wait_send()
            out_send(2 * i).wait_send()
            return 0

        lax.fori_loop(1, chips, step, 0)

    @pl.when(first_core)
    def _():
        y_send(row + 1).wait_send()
        out_send(row + 1).wait_send()


def solution(mesh):
    rows_n, cols_n = mesh.shape["prow"], mesh.shape["pcol"]

    def on_device(factor_t, pattern, diag_inverse, right_side, later_solution):
        panels, narrow, _ = factor_t.shape
        width = diag_inverse.shape[2]
        rhs = right_side.shape[1]
        pairs = panels * (panels - 1) // 2
        side = math.isqrt(cols_n)
        group, quarter = side * narrow, side * width
        own = rhs // cols_n
        dma = pltpu.SemaphoreType.DMA
        per_col, per_row, per_side = dma((cols_n,)), dma((rows_n,)), dma((side,))
        vmem = pltpu.VMEM
        scratch = [
            vmem((panels, group, quarter), BF16),
            vmem((quarter, rhs), BF16),
            vmem((panels, width, width), BF16),
            vmem((pairs, narrow, width), BF16),
            vmem((pairs, width, width), BF16),
            vmem((cols_n, own, width), BF16),
            vmem((own, width), BF16),
            vmem((panels, own, width), BF16),
            vmem((cols_n, own, panels * group), BF16),
            vmem((cols_n, own, panels * group), BF16),
            vmem((panels, own, width), BF16),
            vmem((rows_n, panels, own, width), BF16),
            vmem((side, own, panels * group), BF16),
            vmem((panels, own, width), BF16),
            vmem((cols_n, own, panels * group), BF16),
            vmem((side, rhs, width), BF16),
            vmem((side, rhs, width), BF16),
            vmem((panels, width, 128), BF16),
            vmem((cols_n, panels, narrow, 128), BF16),
            vmem((panels, narrow, rhs), BF16),
            vmem(right_side.shape, BF16),
            vmem((panels * group, rhs), F32),
            pltpu.SMEM((panels, pattern.shape[0]), jnp.int32),
            dma((8,)),
            pltpu.SemaphoreType.REGULAR,
            per_side, per_side,
            per_side, per_side,
            per_col, per_col,
            dma, dma((panels,)),
            per_col, per_col,
            per_col, dma,
            dma, dma((panels,)),
            per_col, per_col,
            dma, per_row,
            per_row, dma,
            per_col, per_col,
            per_side, per_side,
            per_col, per_col,
            per_row, dma,
        ]

        def stay(operand):
            return pltpu.with_memory_space_constraint(operand, pltpu.MemorySpace.HBM)

        anywhere = pl.BlockSpec(memory_space=pltpu.MemorySpace.HBM)
        return pl.pallas_call(
            lambda *refs: kernel(rows_n, cols_n, panels, width, *refs),
            out_shape=(
                jax.ShapeDtypeStruct((panels, narrow, rhs), BF16),
                jax.ShapeDtypeStruct(right_side.shape, BF16),
            ),
            in_specs=[anywhere] * 5,
            out_specs=(
                pl.BlockSpec(memory_space=pltpu.VMEM),
                pl.BlockSpec(memory_space=pltpu.VMEM),
            ),
            scratch_shapes=scratch,
            compiler_params=pltpu.CompilerParams(
                collective_id=0, has_side_effects=True, vmem_limit_bytes=48 << 20
            ),
            name="solve",
        )(stay(factor_t), stay(pattern.T), stay(diag_inverse), stay(right_side), stay(later_solution))

    in_specs = (
        P(None, "pcol", "prow"),
        P("prow", None),
        P(None, "pcol", None),
        P(("prow", "pcol"), None),
        P(("prow", "pcol"), None),
    )
    out_specs = (P(None, "pcol", None), P(("prow", "pcol"), None))
    return jax.shard_map(
        on_device, mesh=mesh, in_specs=in_specs, out_specs=out_specs, check_vma=False
    )
```

```python
import math

import jax
import jax.numpy as jnp
from jax import lax
from jax.experimental import pallas as pl
from jax.experimental.pallas import tpu as pltpu
from jax.sharding import PartitionSpec as P

ROOT = 1
F32 = jnp.float32
BF16 = jnp.bfloat16


def dot(a, b, ca=1, cb=0):
    return lax.dot_general(a, b, (((ca,), (cb,)), ((), ())), preferred_element_type=F32)


def remote(src, dst, send_sem, recv_sem, **device):
    return pltpu.make_async_remote_copy(
        src_ref=src,
        dst_ref=dst,
        send_sem=send_sem,
        recv_sem=recv_sem,
        device_id=device,
        device_id_type=pl.DeviceIdType.MESH,
    )


def signal(sem, **device):
    pl.semaphore_signal(sem, inc=1, device_id=device, device_id_type=pl.DeviceIdType.MESH)


def kernel(rows_n, cols_n, panels, width, *refs):
    factor, pattern_in, diag, right, later, sol_out, red_out = refs[:7]
    (
        part, later_all, inv, lead_own, lead, rt_slabs, rt_own, rt_all, bulk, bulk_in, z_own,
        z_in, y_own, y_keep, y_all, low, low_in, spread, sol_in, out_buf, right_v, acc, pattern,
    ) = refs[7:30]
    (
        loc, hello, fa, fb, ha, hb, da, db, la, lb, ga, gb, ra, rb, qa, qb, sa, sb, za, zb,
        ya, yb, va, vb, wa, wb, ta, tb, oa, ob,
    ) = refs[30:]
    row = lax.axis_index("prow")
    col = lax.axis_index("pcol")
    side = math.isqrt(cols_n)
    x, y = lax.div(col, side), lax.rem(col, side)
    narrow = width // cols_n
    group = side * narrow
    quarter = side * width
    is_root = row == ROOT

    fetch = pltpu.make_async_copy(right, right_v, loc.at[0])
    fetch.start()
    fetch_pattern = pltpu.make_async_copy(pattern_in, pattern, loc.at[5])
    fetch_pattern.start()

    barrier = pltpu.get_barrier_semaphore()

    def greet_col(i, _):
        signal(barrier, pcol=lax.rem(col + i, cols_n))
        return 0

    def greet_row(i, _):
        signal(barrier, prow=lax.rem(row + i, rows_n))
        return 0

    lax.fori_loop(1, cols_n, greet_col, 0)
    @pl.when(is_root)
    def _():
        lax.fori_loop(1, rows_n, greet_row, 0)

    beside = row + 1 - 2 * lax.rem(row, 2)
    same_core = lax.rem(row, 2) == ROOT % 2

    @pl.when(lax.rem(row, 2) != ROOT % 2)
    def _():
        signal(barrier, prow=beside)

    expected = cols_n - 1 + jnp.where(is_root, 0, 1) + jnp.where(same_core, 1, 0)
    pl.semaphore_wait(barrier, expected)

    def strip(ref, j):
        return ref.at[:, pl.ds(pl.multiple_of(j * narrow, narrow), narrow), :]

    class Exchange:
        def __init__(self, count, peer, src, dst, send, recv, me):
            self.count, self.peer, self.src, self.dst = count, peer, src, dst
            self.send, self.recv, self.me = send, recv, me

        def each(self, what):
            def step(i, _):
                device, j = self.peer(i)
                to = self.me if what == "start" else j
                getattr(
                    remote(
                        self.src(j), self.dst(to), self.send.at[i], self.recv.at[to], pcol=device
                    ),
                    what,
                )()
                return 0

            lax.fori_loop(1, self.count, step, 0)

        def start(self):
            self.each("start")

        def arrive(self):
            self.each("wait_recv")

        def drain(self):
            self.each("wait_send")

    def any_peer(i):
        at = lax.rem(i + cols_n // 2 + side // 2 - 1, cols_n)
        at = jnp.where(at < cols_n // 2 + side // 2 - 1, at + 1, at)
        jx = lax.rem(x + lax.div(at, side), side)
        jy = lax.rem(y + lax.rem(at, side), side)
        return jx * side + jy, jx * side + jy

    def x_peer(i):
        j = lax.rem(x + i, side)
        return j * side + y, j

    def y_peer(i):
        j = lax.rem(y + i, side)
        return x * side + j, j

    def over_all(src, dst, send, recv):
        return Exchange(cols_n, any_peer, src, dst, send, recv, col)

    def turned(j):
        return lax.rem(j, side) * side + lax.div(j, side)

    def factor_quarter(j):
        return factor.at[:, :, pl.ds(pl.multiple_of(j * quarter, quarter), quarter)]

    def later_strip(j):
        return later_all.at[pl.ds(pl.multiple_of(j * width, width), width), :]

    factor_x = Exchange(
        side, x_peer, factor_quarter, lambda j: strip(part, j), fa, fb, x
    )
    later_x = Exchange(side, y_peer, lambda j: later, later_strip, ha, hb, y)
    inv_x = over_all(lambda j: diag, lambda j: strip(inv, turned(j)), da, db)
    lead_x = over_all(lambda j: lead_own, lambda j: strip(lead, turned(j)), ga, gb)
    bulk_x = over_all(lambda j: bulk.at[j], lambda j: bulk_in.at[j], sa, sb)
    y_x = over_all(lambda j: y_own.at[lax.rem(j, side)], lambda j: y_all.at[j], va, vb)
    low_x = Exchange(
        side, y_peer, lambda j: low.at[j], lambda j: low_in.at[j], wa, wb, y
    )
    sol_x = over_all(lambda j: strip(spread, j), lambda j: sol_in.at[j], ta, tb)

    def lead_copy(q):
        first = q * (q - 1) // 2
        return remote(
            factor.at[pl.ds(0, q), :, pl.ds(0, width)],
            lead_own.at[pl.ds(first, q)],
            la,
            lb.at[q],
            prow=ROOT,
        )

    def lead_here():
        first = ROOT * (ROOT - 1) // 2
        return pltpu.make_async_copy(
            factor.at[pl.ds(0, ROOT), :, pl.ds(0, width)],
            lead_own.at[pl.ds(first, ROOT)],
            loc.at[6],
        )

    for q in range(1, panels):

        @pl.when(row == q)
        def _(q=q):
            (lead_here() if q == ROOT else lead_copy(q)).start()

    @pl.when(is_root)
    def _():
        inv_x.start()
        pltpu.make_async_copy(diag, strip(inv, turned(col)), loc.at[3]).start()

    factor_x.start()
    later_x.start()
    own_copies = [
        pltpu.make_async_copy(factor_quarter(x), strip(part, x), loc.at[1]),
        pltpu.make_async_copy(later, later_strip(y), loc.at[2]),
    ]
    for copy in own_copies:
        copy.start()

    @pl.when(row != ROOT)
    def _():
        signal(hello, prow=ROOT)

    fetch.wait()
    fetch_pattern.wait()

    def rt_scatter(j):
        return remote(rt_slabs.at[j], rt_own, ra.at[j], rb, pcol=j)

    @pl.when((row < panels) & (col == 0))
    def _():
        flipped = right_v[...].astype(F32).T.astype(BF16)
        rt_slabs[...] = flipped.reshape(rt_slabs.shape)

        def step(j, _):
            rt_scatter(j).start()
            return 0

        lax.fori_loop(1, cols_n, step, 0)
        rt_own[...] = rt_slabs[0]

    @pl.when((row < panels) & (col != 0))
    def _():
        rt_scatter(0).wait_recv()

    def rt_send(q):
        return remote(rt_own, rt_all.at[q], qa, qb.at[q], prow=ROOT)

    others = [q for q in range(panels) if q != ROOT]
    for q in others:

        @pl.when(row == q)
        def _(q=q):
            rt_send(q).start()

    @pl.when(is_root)
    def _():
        rt_all[ROOT] = rt_own[...]
        for q in range(1, panels):
            if q == ROOT:
                lead_here().wait()
            else:
                lead_copy(q).wait_recv()

        lead_x.start()
        pltpu.make_async_copy(lead_own, strip(lead, turned(col)), loc.at[4]).start()

    factor_x.arrive()
    later_x.arrive()
    for copy in own_copies:
        copy.wait()
    columns = panels * group

    @pl.when((row < panels) & (x == 0))
    def _():
        later_all[:width, :] = jnp.zeros((width, later_all.shape[1]), BF16)

    acc[...] = jnp.zeros_like(acc)

    def block_of(b):
        return pl.ds(pl.multiple_of(b * width, width), width)

    def bulk_step(b, _):
        rows = block_of(b)
        pieces = []
        for p in range(panels):
            keep = pattern[p, x * side + b].astype(F32).astype(BF16)
            piece = part[p, :, rows] * keep
            part[p, :, rows] = piece
            pieces.append(piece)
        acc[...] += dot(jnp.concatenate(pieces, axis=0), later_all[rows, :])
        return 0

    lax.fori_loop(0, side, bulk_step, 0)
    bulk[...] = acc[...].T.astype(BF16).reshape(bulk.shape)
    bulk_x.start()
    bulk_in[col] = bulk[col]

    chips = rows_n // 2

    def along_row(send):
        def step(i, _):
            send(lax.rem(ROOT + 2 * i, rows_n)).start()
            return 0

        lax.fori_loop(1, chips, step, 0)
        send(beside).start()

    relays = same_core & (row != ROOT)

    def y_send(r):
        return remote(y_own, y_own, ya.at[r], yb, prow=r)

    @pl.when(is_root)
    def _():
        inv_x.arrive()
        pltpu.make_async_copy(diag, strip(inv, turned(col)), loc.at[3]).wait()
        lead_x.arrive()
        pltpu.make_async_copy(lead_own, strip(lead, turned(col)), loc.at[4]).wait()
        solved = []
        for q in range(panels):
            if q != ROOT:
                rt_send(q).wait_recv()
            residual = rt_all[q].astype(F32)
            for p in range(q):
                residual = residual - dot(solved[p], lead[q * (q - 1) // 2 + p])
            y_q = dot(residual.astype(BF16), inv[q], 1, 1).astype(BF16)
            solved.append(y_q)
            y_keep[q] = y_q
        for j in range(side):
            pieces = [y_q[:, j * group : (j + 1) * group] for y_q in solved]
            y_own[j] = jnp.concatenate(pieces, axis=1)
        y_x.start()
        pl.semaphore_wait(hello, rows_n - 1)
        along_row(y_send)

    bulk_x.arrive()
    def sum_step(i, sums):
        return tuple(t + bulk_in[i * side + j].astype(F32) for j, t in enumerate(sums))

    sums = lax.fori_loop(
        1, side, sum_step, tuple(bulk_in[j].astype(F32) for j in range(side))
    )
    for p in range(panels):
        pieces = [total[:, p * group : (p + 1) * group] for total in sums]
        z_own[p] = jnp.concatenate(pieces, axis=1).astype(z_own.dtype)

    def z_send(r):
        return remote(z_own, z_in.at[r], za, zb.at[r], prow=ROOT)

    @pl.when(row != ROOT)
    def _():
        z_send(row).start()
        y_send(ROOT).wait_recv()

        @pl.when(relays)
        def _():
            y_send(beside).start()

        y_x.start()

    y_all[col] = y_own[y]
    y_x.arrive()

    def lower_step(j, _):
        strip_j = part[:, :, block_of(j)].reshape(columns, width)
        low[j] = dot(y_all[...].reshape(-1, columns), strip_j).astype(BF16)
        return 0

    lax.fori_loop(0, side, lower_step, 0)
    low_x.start()
    low_in[y] = low[y]

    def out_send(r):
        return remote(out_buf, out_buf, oa.at[r], ob, prow=r)

    @pl.when(is_root)
    def _():
        def gather_step(r, sums):
            sender = lax.rem(ROOT + r, rows_n)
            z_send(sender).wait_recv()
            return tuple(t + z_in[sender, p].astype(F32) for p, t in enumerate(sums))

        gathered = lax.fori_loop(
            1, rows_n, gather_step, tuple(z_own[p].astype(F32) for p in range(panels))
        )
        answers = [None] * panels
        shift = lax.rem(col, cols_n // 2) * narrow
        shape = (narrow, 128)
        at = lax.broadcasted_iota(jnp.int32, shape, 0) + shift
        place = (lax.broadcasted_iota(jnp.int32, shape, 1) == at).astype(BF16)
        for p in reversed(range(panels)):
            column = gathered[p]
            for q in range(panels - 1, p, -1):
                column = column + dot(answers[q], lead[q * (q - 1) // 2 + p], 1, 1)
            gap = y_keep[p].astype(F32) - column
            high = gap.astype(BF16)
            rest = gap - high.astype(F32)
            middle = rest.astype(BF16)
            lowest = (rest - middle.astype(F32)).astype(BF16)
            parts = dot(jnp.concatenate([high, middle, lowest], axis=0), inv[p])
            applied = parts[:narrow] + (parts[narrow : 2 * narrow] + parts[2 * narrow :])
            answers[p] = applied.astype(BF16)
            spread[p] = dot(answers[p], place, 0, 0).astype(BF16)
        sol_x.start()
        mine = pl.ds(pl.multiple_of(col * narrow, narrow), narrow)
        sol_in[col] = spread[:, mine, :]

    @pl.when(is_root)
    def _():
        sol_x.arrive()
        half = cols_n // 2

        def merge_step(j, sums):
            first, second = sums
            return first + sol_in[j].astype(F32), second + sol_in[half + j].astype(F32)

        merged = lax.fori_loop(
            1, half, merge_step, (sol_in[0].astype(F32), sol_in[half].astype(F32))
        )
        out_buf[:, :, :128] = merged[0].astype(BF16)
        out_buf[:, :, 128:] = merged[1].astype(BF16)

        along_row(out_send)

    low_x.arrive()
    lower_t = low_in[0].astype(F32)
    for j in range(1, side):
        lower_t = lower_t + low_in[j].astype(F32)
    red_out[...] = (right_v[...].astype(F32) - lower_t.T).astype(BF16)

    @pl.when(row != ROOT)
    def _():
        out_send(ROOT).wait_recv()

        @pl.when(relays)
        def _():
            out_send(beside).start()

    sol_out[...] = out_buf[...]

    for exchange in (factor_x, later_x, bulk_x, y_x, low_x):
        exchange.drain()

    @pl.when((row < panels) & (col == 0))
    def _():
        def step(j, _):
            rt_scatter(j).wait_send()
            return 0

        lax.fori_loop(1, cols_n, step, 0)

    for q in others:

        @pl.when(row == q)
        def _(q=q):
            if q > 0:
                lead_copy(q).wait_send()
            rt_send(q).wait_send()

    @pl.when(row != ROOT)
    def _():
        z_send(row).wait_send()

    @pl.when(is_root)
    def _():
        inv_x.drain()
        lead_x.drain()
        sol_x.drain()

        def step(i, _):
            to = lax.rem(ROOT + 2 * i, rows_n)
            y_send(to).wait_send()
            out_send(to).wait_send()
            return 0

        lax.fori_loop(1, chips, step, 0)

    @pl.when(same_core)
    def _():
        y_send(beside).wait_send()
        out_send(beside).wait_send()


def solution(mesh):
    rows_n, cols_n = mesh.shape["prow"], mesh.shape["pcol"]

    def on_device(factor_t, pattern, diag_inverse, right_side, later_solution):
        panels, narrow, _ = factor_t.shape
        width = diag_inverse.shape[2]
        rhs = right_side.shape[1]
        pairs = panels * (panels - 1) // 2
        side = math.isqrt(cols_n)
        group, quarter = side * narrow, side * width
        own = rhs // cols_n
        dma = pltpu.SemaphoreType.DMA
        per_col, per_row, per_side = dma((cols_n,)), dma((rows_n,)), dma((side,))
        vmem = pltpu.VMEM
        scratch = [
            vmem((panels, group, quarter), BF16),
            vmem((quarter, rhs), BF16),
            vmem((panels, width, width), BF16),
            vmem((pairs, narrow, width), BF16),
            vmem((pairs, width, width), BF16),
            vmem((cols_n, own, width), BF16),
            vmem((own, width), BF16),
            vmem((panels, own, width), BF16),
            vmem((cols_n, own, panels * group), BF16),
            vmem((cols_n, own, panels * group), BF16),
            vmem((panels, own, width), BF16),
            vmem((rows_n, panels, own, width), BF16),
            vmem((side, own, panels * group), BF16),
            vmem((panels, own, width), BF16),
            vmem((cols_n, own, panels * group), BF16),
            vmem((side, rhs, width), BF16),
            vmem((side, rhs, width), BF16),
            vmem((panels, width, 128), BF16),
            vmem((cols_n, panels, narrow, 128), BF16),
            vmem((panels, narrow, rhs), BF16),
            vmem(right_side.shape, BF16),
            vmem((panels * group, rhs), F32),
            pltpu.SMEM((panels, pattern.shape[0]), jnp.int32),
            dma((8,)),
            pltpu.SemaphoreType.REGULAR,
            per_side, per_side,
            per_side, per_side,
            per_col, per_col,
            dma, dma((panels,)),
            per_col, per_col,
            per_col, dma,
            dma, dma((panels,)),
            per_col, per_col,
            dma, per_row,
            per_row, dma,
            per_col, per_col,
            per_side, per_side,
            per_col, per_col,
            per_row, dma,
        ]

        def stay(operand):
            return pltpu.with_memory_space_constraint(operand, pltpu.MemorySpace.HBM)

        anywhere = pl.BlockSpec(memory_space=pltpu.MemorySpace.HBM)
        return pl.pallas_call(
            lambda *refs: kernel(rows_n, cols_n, panels, width, *refs),
            out_shape=(
                jax.ShapeDtypeStruct((panels, narrow, rhs), BF16),
                jax.ShapeDtypeStruct(right_side.shape, BF16),
            ),
            in_specs=[anywhere] * 5,
            out_specs=(
                pl.BlockSpec(memory_space=pltpu.VMEM),
                pl.BlockSpec(memory_space=pltpu.VMEM),
            ),
            scratch_shapes=scratch,
            compiler_params=pltpu.CompilerParams(
                collective_id=0, has_side_effects=True, vmem_limit_bytes=48 << 20
            ),
            name="solve",
        )(stay(factor_t), stay(pattern.T), stay(diag_inverse), stay(right_side), stay(later_solution))

    in_specs = (
        P(None, "pcol", "prow"),
        P("prow", None),
        P(None, "pcol", None),
        P(("prow", "pcol"), None),
        P(("prow", "pcol"), None),
    )
    out_specs = (P(None, "pcol", None), P(("prow", "pcol"), None))
    return jax.shard_map(
        on_device, mesh=mesh, in_specs=in_specs, out_specs=out_specs, check_vma=False
    )
```

```python
import math

import jax
import jax.numpy as jnp
from jax import lax
from jax.experimental import pallas as pl
from jax.experimental.pallas import tpu as pltpu
from jax.sharding import PartitionSpec as P

ROOT = 1
F32 = jnp.float32
BF16 = jnp.bfloat16


def dot(a, b, ca=1, cb=0):
    return lax.dot_general(a, b, (((ca,), (cb,)), ((), ())), preferred_element_type=F32)


def remote(src, dst, send_sem, recv_sem, **device):
    return pltpu.make_async_remote_copy(
        src_ref=src,
        dst_ref=dst,
        send_sem=send_sem,
        recv_sem=recv_sem,
        device_id=device,
        device_id_type=pl.DeviceIdType.MESH,
    )


def signal(sem, **device):
    pl.semaphore_signal(sem, inc=1, device_id=device, device_id_type=pl.DeviceIdType.MESH)


def kernel(rows_n, cols_n, panels, width, *refs):
    factor, pattern_in, diag, right, later, sol_out, red_out = refs[:7]
    (
        part, later_all, inv, lead_own, lead, rt_slabs, rt_own, rt_all, bulk, bulk_in, z_own,
        z_in, y_own, y_keep, y_all, low, low_in, spread, sol_in, out_buf, right_v, acc, pattern,
    ) = refs[7:30]
    (
        loc, hello, fa, fb, ha, hb, da, db, la, lb, ga, gb, ra, rb, qa, qb, sa, sb, za, zb,
        ya, yb, va, vb, wa, wb, ta, tb, oa, ob,
    ) = refs[30:]
    row = lax.axis_index("prow")
    col = lax.axis_index("pcol")
    side = math.isqrt(cols_n)
    x, y = lax.div(col, side), lax.rem(col, side)
    narrow = width // cols_n
    group = side * narrow
    quarter = side * width
    is_root = row == ROOT

    fetch = pltpu.make_async_copy(right, right_v, loc.at[0])
    fetch.start()
    fetch_pattern = pltpu.make_async_copy(pattern_in, pattern, loc.at[5])
    fetch_pattern.start()

    barrier = pltpu.get_barrier_semaphore()

    def greet_col(i, _):
        signal(barrier, pcol=lax.rem(col + i, cols_n))
        return 0

    def greet_row(i, _):
        signal(barrier, prow=lax.rem(row + i, rows_n))
        return 0

    lax.fori_loop(1, cols_n, greet_col, 0)
    @pl.when(is_root)
    def _():
        lax.fori_loop(1, rows_n, greet_row, 0)

    beside = row + 1 - 2 * lax.rem(row, 2)
    same_core = lax.rem(row, 2) == ROOT % 2

    @pl.when(lax.rem(row, 2) != ROOT % 2)
    def _():
        signal(barrier, prow=beside)

    expected = cols_n - 1 + jnp.where(is_root, 0, 1) + jnp.where(same_core, 1, 0)
    pl.semaphore_wait(barrier, expected)

    def strip(ref, j):
        return ref.at[:, pl.ds(pl.multiple_of(j * narrow, narrow), narrow), :]

    class Exchange:
        def __init__(self, count, peer, src, dst, send, recv, me):
            self.count, self.peer, self.src, self.dst = count, peer, src, dst
            self.send, self.recv, self.me = send, recv, me

        def each(self, what):
            def step(i, _):
                device, j = self.peer(i)
                to = self.me if what == "start" else j
                getattr(
                    remote(
                        self.src(j), self.dst(to), self.send.at[i], self.recv.at[to], pcol=device
                    ),
                    what,
                )()
                return 0

            lax.fori_loop(1, self.count, step, 0)

        def start(self):
            self.each("start")

        def arrive(self):
            self.each("wait_recv")

        def drain(self):
            self.each("wait_send")

    def any_peer(i):
        at = lax.rem(i + cols_n // 2 + side // 2 - 1, cols_n)
        at = jnp.where(at < cols_n // 2 + side // 2 - 1, at + 1, at)
        jx = lax.rem(x + lax.div(at, side), side)
        jy = lax.rem(y + lax.rem(at, side), side)
        return jx * side + jy, jx * side + jy

    def x_peer(i):
        j = lax.rem(x + i, side)
        return j * side + y, j

    def y_peer(i):
        j = lax.rem(y + i, side)
        return x * side + j, j

    def over_all(src, dst, send, recv):
        return Exchange(cols_n, any_peer, src, dst, send, recv, col)

    def turned(j):
        return lax.rem(j, side) * side + lax.div(j, side)

    def factor_quarter(j):
        return factor.at[:, :, pl.ds(pl.multiple_of(j * quarter, quarter), quarter)]

    def later_strip(j):
        return later_all.at[pl.ds(pl.multiple_of(j * width, width), width), :]

    factor_x = Exchange(
        side, x_peer, factor_quarter, lambda j: strip(part, j), fa, fb, x
    )
    later_x = Exchange(side, y_peer, lambda j: later, later_strip, ha, hb, y)
    inv_x = over_all(lambda j: diag, lambda j: strip(inv, turned(j)), da, db)
    lead_x = over_all(lambda j: lead_own, lambda j: strip(lead, turned(j)), ga, gb)
    bulk_x = over_all(lambda j: bulk.at[j], lambda j: bulk_in.at[j], sa, sb)
    y_x = over_all(lambda j: y_own.at[lax.rem(j, side)], lambda j: y_all.at[j], va, vb)
    low_x = Exchange(
        side, y_peer, lambda j: low.at[j], lambda j: low_in.at[j], wa, wb, y
    )
    sol_x = over_all(lambda j: strip(spread, j), lambda j: sol_in.at[j], ta, tb)

    def lead_copy(q):
        first = q * (q - 1) // 2
        return remote(
            factor.at[pl.ds(0, q), :, pl.ds(0, width)],
            lead_own.at[pl.ds(first, q)],
            la,
            lb.at[q],
            prow=ROOT,
        )

    def lead_here():
        first = ROOT * (ROOT - 1) // 2
        return pltpu.make_async_copy(
            factor.at[pl.ds(0, ROOT), :, pl.ds(0, width)],
            lead_own.at[pl.ds(first, ROOT)],
            loc.at[6],
        )

    for q in range(1, panels):

        @pl.when(row == q)
        def _(q=q):
            (lead_here() if q == ROOT else lead_copy(q)).start()

    @pl.when(is_root)
    def _():
        inv_x.start()
        pltpu.make_async_copy(diag, strip(inv, turned(col)), loc.at[3]).start()

    factor_x.start()
    later_x.start()
    own_copies = [
        pltpu.make_async_copy(factor_quarter(x), strip(part, x), loc.at[1]),
        pltpu.make_async_copy(later, later_strip(y), loc.at[2]),
    ]
    for copy in own_copies:
        copy.start()

    @pl.when(row != ROOT)
    def _():
        signal(hello, prow=ROOT)

    fetch.wait()
    fetch_pattern.wait()

    def rt_scatter(j):
        return remote(rt_slabs.at[j], rt_own, ra.at[j], rb, pcol=j)

    @pl.when((row < panels) & (col == 0))
    def _():
        flipped = right_v[...].astype(F32).T.astype(BF16)
        rt_slabs[...] = flipped.reshape(rt_slabs.shape)

        def step(j, _):
            rt_scatter(j).start()
            return 0

        lax.fori_loop(1, cols_n, step, 0)
        rt_own[...] = rt_slabs[0]

    @pl.when((row < panels) & (col != 0))
    def _():
        rt_scatter(0).wait_recv()

    def rt_send(q):
        return remote(rt_own, rt_all.at[q], qa, qb.at[q], prow=ROOT)

    others = [q for q in range(panels) if q != ROOT]
    for q in others:

        @pl.when(row == q)
        def _(q=q):
            rt_send(q).start()

    @pl.when(is_root)
    def _():
        rt_all[ROOT] = rt_own[...]
        for q in range(1, panels):
            if q == ROOT:
                lead_here().wait()
            else:
                lead_copy(q).wait_recv()

        lead_x.start()
        pltpu.make_async_copy(lead_own, strip(lead, turned(col)), loc.at[4]).start()

    factor_x.arrive()
    later_x.arrive()
    for copy in own_copies:
        copy.wait()
    columns = panels * group

    @pl.when((row < panels) & (x == 0))
    def _():
        later_all[:width, :] = jnp.zeros((width, later_all.shape[1]), BF16)

    acc[...] = jnp.zeros_like(acc)

    def block_of(b):
        return pl.ds(pl.multiple_of(b * width, width), width)

    def bulk_step(b, _):
        rows = block_of(b)
        pieces = []
        for p in range(panels):
            keep = pattern[p, x * side + b].astype(F32).astype(BF16)
            piece = part[p, :, rows] * keep
            part[p, :, rows] = piece
            pieces.append(piece)
        acc[...] += dot(jnp.concatenate(pieces, axis=0), later_all[rows, :])
        return 0

    lax.fori_loop(0, side, bulk_step, 0)
    bulk[...] = acc[...].T.astype(BF16).reshape(bulk.shape)
    bulk_x.start()
    bulk_in[col] = bulk[col]

    chips = rows_n // 2

    def along_row(send):
        def step(i, _):
            send(lax.rem(ROOT + 2 * i, rows_n)).start()
            return 0

        lax.fori_loop(1, chips, step, 0)
        send(beside).start()

    relays = same_core & (row != ROOT)

    def y_send(r):
        return remote(y_own, y_own, ya.at[r], yb, prow=r)

    @pl.when(is_root)
    def _():
        inv_x.arrive()
        pltpu.make_async_copy(diag, strip(inv, turned(col)), loc.at[3]).wait()
        lead_x.arrive()
        pltpu.make_async_copy(lead_own, strip(lead, turned(col)), loc.at[4]).wait()
        solved = []
        for q in range(panels):
            if q != ROOT:
                rt_send(q).wait_recv()
            residual = rt_all[q].astype(F32)
            for p in range(q):
                residual = residual - dot(solved[p], lead[q * (q - 1) // 2 + p])
            y_q = dot(residual.astype(BF16), inv[q], 1, 1).astype(BF16)
            solved.append(y_q)
            y_keep[q] = y_q
        for j in range(side):
            pieces = [y_q[:, j * group : (j + 1) * group] for y_q in solved]
            y_own[j] = jnp.concatenate(pieces, axis=1)
        y_x.start()
        pl.semaphore_wait(hello, rows_n - 1)
        along_row(y_send)

    bulk_x.arrive()
    def sum_step(i, sums):
        return tuple(t + bulk_in[i * side + j].astype(F32) for j, t in enumerate(sums))

    sums = lax.fori_loop(
        1, side, sum_step, tuple(bulk_in[j].astype(F32) for j in range(side))
    )
    for p in range(panels):
        pieces = [total[:, p * group : (p + 1) * group] for total in sums]
        z_own[p] = jnp.concatenate(pieces, axis=1).astype(z_own.dtype)

    def z_send(r):
        return remote(z_own, z_in.at[r], za, zb.at[r], prow=ROOT)

    @pl.when(row != ROOT)
    def _():
        z_send(row).start()
        y_send(ROOT).wait_recv()

        @pl.when(relays)
        def _():
            y_send(beside).start()

        y_x.start()

    y_all[col] = y_own[y]
    y_x.arrive()

    def lower_strip(j):
        strip_j = part[:, :, block_of(j)].reshape(columns, width)
        low[j] = dot(y_all[...].reshape(-1, columns), strip_j).astype(BF16)

    def lower_step(i, _):
        device, j = y_peer(i)
        lower_strip(j)
        remote(low.at[j], low_in.at[y], wa.at[i], wb.at[y], pcol=device).start()
        return 0

    lax.fori_loop(1, side, lower_step, 0)
    lower_strip(y)
    low_in[y] = low[y]

    def out_send(r):
        return remote(out_buf, out_buf, oa.at[r], ob, prow=r)

    @pl.when(is_root)
    def _():
        def gather_step(r, sums):
            sender = lax.rem(ROOT + r, rows_n)
            z_send(sender).wait_recv()
            return tuple(t + z_in[sender, p].astype(F32) for p, t in enumerate(sums))

        gathered = lax.fori_loop(
            1, rows_n, gather_step, tuple(z_own[p].astype(F32) for p in range(panels))
        )
        answers = [None] * panels
        shift = lax.rem(col, cols_n // 2) * narrow
        shape = (narrow, 128)
        at = lax.broadcasted_iota(jnp.int32, shape, 0) + shift
        place = (lax.broadcasted_iota(jnp.int32, shape, 1) == at).astype(BF16)
        for p in reversed(range(panels)):
            column = gathered[p]
            for q in range(panels - 1, p, -1):
                column = column + dot(answers[q], lead[q * (q - 1) // 2 + p], 1, 1)
            gap = y_keep[p].astype(F32) - column
            high = gap.astype(BF16)
            rest = gap - high.astype(F32)
            middle = rest.astype(BF16)
            lowest = (rest - middle.astype(F32)).astype(BF16)
            parts = dot(jnp.concatenate([high, middle, lowest], axis=0), inv[p])
            applied = parts[:narrow] + (parts[narrow : 2 * narrow] + parts[2 * narrow :])
            answers[p] = applied.astype(BF16)
            spread[p] = dot(answers[p], place, 0, 0).astype(BF16)
        sol_x.start()
        mine = pl.ds(pl.multiple_of(col * narrow, narrow), narrow)
        sol_in[col] = spread[:, mine, :]

    @pl.when(is_root)
    def _():
        sol_x.arrive()
        half = cols_n // 2

        def merge_step(j, sums):
            first, second = sums
            return first + sol_in[j].astype(F32), second + sol_in[half + j].astype(F32)

        merged = lax.fori_loop(
            1, half, merge_step, (sol_in[0].astype(F32), sol_in[half].astype(F32))
        )
        out_buf[:, :, :128] = merged[0].astype(BF16)
        out_buf[:, :, 128:] = merged[1].astype(BF16)

        along_row(out_send)

    low_x.arrive()
    lower_t = low_in[0].astype(F32)
    for j in range(1, side):
        lower_t = lower_t + low_in[j].astype(F32)
    red_out[...] = (right_v[...].astype(F32) - lower_t.T).astype(BF16)

    @pl.when(row != ROOT)
    def _():
        out_send(ROOT).wait_recv()

        @pl.when(relays)
        def _():
            out_send(beside).start()

    sol_out[...] = out_buf[...]

    for exchange in (factor_x, later_x, bulk_x, y_x, low_x):
        exchange.drain()

    @pl.when((row < panels) & (col == 0))
    def _():
        def step(j, _):
            rt_scatter(j).wait_send()
            return 0

        lax.fori_loop(1, cols_n, step, 0)

    for q in others:

        @pl.when(row == q)
        def _(q=q):
            if q > 0:
                lead_copy(q).wait_send()
            rt_send(q).wait_send()

    @pl.when(row != ROOT)
    def _():
        z_send(row).wait_send()

    @pl.when(is_root)
    def _():
        inv_x.drain()
        lead_x.drain()
        sol_x.drain()

        def step(i, _):
            to = lax.rem(ROOT + 2 * i, rows_n)
            y_send(to).wait_send()
            out_send(to).wait_send()
            return 0

        lax.fori_loop(1, chips, step, 0)

    @pl.when(same_core)
    def _():
        y_send(beside).wait_send()
        out_send(beside).wait_send()


def solution(mesh):
    rows_n, cols_n = mesh.shape["prow"], mesh.shape["pcol"]

    def on_device(factor_t, pattern, diag_inverse, right_side, later_solution):
        panels, narrow, _ = factor_t.shape
        width = diag_inverse.shape[2]
        rhs = right_side.shape[1]
        pairs = panels * (panels - 1) // 2
        side = math.isqrt(cols_n)
        group, quarter = side * narrow, side * width
        own = rhs // cols_n
        dma = pltpu.SemaphoreType.DMA
        per_col, per_row, per_side = dma((cols_n,)), dma((rows_n,)), dma((side,))
        vmem = pltpu.VMEM
        scratch = [
            vmem((panels, group, quarter), BF16),
            vmem((quarter, rhs), BF16),
            vmem((panels, width, width), BF16),
            vmem((pairs, narrow, width), BF16),
            vmem((pairs, width, width), BF16),
            vmem((cols_n, own, width), BF16),
            vmem((own, width), BF16),
            vmem((panels, own, width), BF16),
            vmem((cols_n, own, panels * group), BF16),
            vmem((cols_n, own, panels * group), BF16),
            vmem((panels, own, width), BF16),
            vmem((rows_n, panels, own, width), BF16),
            vmem((side, own, panels * group), BF16),
            vmem((panels, own, width), BF16),
            vmem((cols_n, own, panels * group), BF16),
            vmem((side, rhs, width), BF16),
            vmem((side, rhs, width), BF16),
            vmem((panels, width, 128), BF16),
            vmem((cols_n, panels, narrow, 128), BF16),
            vmem((panels, narrow, rhs), BF16),
            vmem(right_side.shape, BF16),
            vmem((panels * group, rhs), F32),
            pltpu.SMEM((panels, pattern.shape[0]), jnp.int32),
            dma((8,)),
            pltpu.SemaphoreType.REGULAR,
            per_side, per_side,
            per_side, per_side,
            per_col, per_col,
            dma, dma((panels,)),
            per_col, per_col,
            per_col, dma,
            dma, dma((panels,)),
            per_col, per_col,
            dma, per_row,
            per_row, dma,
            per_col, per_col,
            per_side, per_side,
            per_col, per_col,
            per_row, dma,
        ]

        def stay(operand):
            return pltpu.with_memory_space_constraint(operand, pltpu.MemorySpace.HBM)

        anywhere = pl.BlockSpec(memory_space=pltpu.MemorySpace.HBM)
        return pl.pallas_call(
            lambda *refs: kernel(rows_n, cols_n, panels, width, *refs),
            out_shape=(
                jax.ShapeDtypeStruct((panels, narrow, rhs), BF16),
                jax.ShapeDtypeStruct(right_side.shape, BF16),
            ),
            in_specs=[anywhere] * 5,
            out_specs=(
                pl.BlockSpec(memory_space=pltpu.VMEM),
                pl.BlockSpec(memory_space=pltpu.VMEM),
            ),
            scratch_shapes=scratch,
            compiler_params=pltpu.CompilerParams(
                collective_id=0, has_side_effects=True, vmem_limit_bytes=48 << 20
            ),
            name="solve",
        )(stay(factor_t), stay(pattern.T), stay(diag_inverse), stay(right_side), stay(later_solution))

    in_specs = (
        P(None, "pcol", "prow"),
        P("prow", None),
        P(None, "pcol", None),
        P(("prow", "pcol"), None),
        P(("prow", "pcol"), None),
    )
    out_specs = (P(None, "pcol", None), P(("prow", "pcol"), None))
    return jax.shard_map(
        on_device, mesh=mesh, in_specs=in_specs, out_specs=out_specs, check_vma=False
    )
```
